256 devices in a mesh: energy: 32 (over z_hi, x, y), cell: 8 (over z_lo, core).
Axes of the slice: x: 4, y: 4, z: 8 (z_hi: 2, z_lo: 4; z = z_hi * 4 + z_lo), core: 2. Of those that a mesh axis runs over, the one named last changes fastest.
Arguments:
- green_pair: float32 [4, 32, 16, 256, 256], P(None, 'energy', 'cell'), may hold values from -4 to 4
- retarded_diag: float32 [2, 32, 16, 256, 256], P(None, 'energy', 'cell'), may hold values from -0.25 to 0.25
- retarded_upper: float32 [2, 32, 16, 256, 256], P(None, 'energy', 'cell'), may hold values from -0.25 to 0.25
- coulomb_diag: float32 [16, 256, 256], P('cell'), may hold values from -0.375 to 0.375
- coulomb_upper: float32 [16, 256, 256], P('cell'), may hold values from -0.375 to 0.375
Outputs:
- lesser_new: float32 [2, 32, 16, 256, 256], P(None, 'energy', 'cell')
The draws below stay inside these ranges and needn't reach their ends.
All inputs are finite; a program needn't handle non-finite values.
Results may differ from the reference program's by a relative error of at most 0.00014.
Values sent between devices are 32-bit elements; how exact they have to be, the bound alone decides.
A program may use at most 64 MiB of HBM per device.

```python
import math
import jax
import jax.numpy as jnp
from jax import lax

B = 256
NE = 32
NC = 16


def level_of(own_key, shape, cuts, least, largest):
    gain = 1.0
    for axis_at, shards_of in cuts:
        draws = jax.random.uniform(jax.random.fold_in(jax.random.fold_in(own_key, 6), axis_at), (shards_of,), jnp.float32, least / len(cuts), largest / len(cuts))
        gain = gain * jnp.repeat(jnp.exp(draws), shape[axis_at] // shards_of).reshape((-1,) + (1,) * (len(shape) - 1 - axis_at))
    return gain


def bell_draw(own_key, dims, width, reach, split=(), held_as=jnp.bfloat16):
    gain = level_of(own_key, dims, split, -0.22, 0.18) if split else 1.0
    values = jax.random.normal(own_key, dims, jnp.float32) * width * gain
    return jnp.minimum(jnp.maximum(values, -reach), reach).astype(held_as)


def setup_inputs(seed: int = 0) -> dict:
    arg_keys = jax.random.split(jax.random.key(seed), 6)
    return {
        "green_pair": bell_draw(arg_keys[0], (4, NE, NC, B, B), 0.5, 4.0, ((1, 32), (2, 8)), jnp.float32),
        "retarded_diag": bell_draw(arg_keys[1], (2, NE, NC, B, B), (2 * B) ** -0.5, 0.25, ((1, 32), (2, 8)), jnp.float32),
        "retarded_upper": bell_draw(arg_keys[2], (2, NE, NC, B, B), (2 * B) ** -0.5, 0.25, ((1, 32), (2, 8)), jnp.float32),
        "coulomb_diag": bell_draw(arg_keys[3], (NC, B, B), B ** -0.5, 0.375, ((0, 8),), jnp.float32),
        "coulomb_upper": bell_draw(arg_keys[4], (NC, B, B), B ** -0.5, 0.375, ((0, 8),), jnp.float32),
    }


highest = lax.Precision.HIGHEST

def shift_prev(values, dimension):
    widths = [(0, 0)] * values.ndim
    widths[dimension] = (1, 0)
    length = values.shape[dimension]
    return lax.slice_in_dim(jnp.pad(values, widths), 0, length, axis=dimension)

def shift_next(values, dimension):
    widths = [(0, 0)] * values.ndim
    widths[dimension] = (0, 1)
    length = values.shape[dimension]
    return lax.slice_in_dim(jnp.pad(values, widths), 1, length + 1, axis=dimension)

def outer_real(left, middle):
    inner = jnp.einsum('cab,ecbd->ecad', left, middle, precision=highest)
    return jnp.einsum('ecad,cfd->ecaf', inner, left, precision=highest)

def outer_complex(left_real, left_imaginary, mid_real, mid_imaginary):
    first_real = jnp.einsum('ecab,ecbd->ecad', left_real, mid_real, precision=highest) - jnp.einsum('ecab,ecbd->ecad', left_imaginary, mid_imaginary, precision=highest)
    first_imaginary = jnp.einsum('ecab,ecbd->ecad', left_real, mid_imaginary, precision=highest) + jnp.einsum('ecab,ecbd->ecad', left_imaginary, mid_real, precision=highest)
    out_real = jnp.einsum('ecad,ecfd->ecaf', first_real, left_real, precision=highest) + jnp.einsum('ecad,ecfd->ecaf', first_imaginary, left_imaginary, precision=highest)
    out_imaginary = jnp.einsum('ecad,ecfd->ecaf', first_imaginary, left_real, precision=highest) - jnp.einsum('ecad,ecfd->ecaf', first_real, left_imaginary, precision=highest)
    return (out_real, out_imaginary)

def reference(green_pair, retarded_diag, retarded_upper, coulomb_diag, coulomb_upper):
    scaling = 1.0 / math.sqrt(NE)
    lesser = green_pair[0] + 1j * green_pair[1]
    greater = green_pair[2] + 1j * green_pair[3]
    lesser_hat = jnp.fft.fft(lesser, axis=0)
    greater_hat = jnp.fft.fft(greater, axis=0)
    correlated = jnp.fft.ifft(lesser_hat * jnp.conj(greater_hat), axis=0)
    pol_real = -jnp.imag(correlated) * scaling
    pol_imaginary = jnp.real(correlated) * scaling
    coulomb_symmetric = (coulomb_diag + jnp.swapaxes(coulomb_diag, 1, 2)) * 0.5
    coulomb_lower = jnp.swapaxes(shift_prev(coulomb_upper, 0), 1, 2)
    screened = []
    for plane in (pol_real, pol_imaginary):
        total = outer_real(coulomb_symmetric, plane)
        total = total + outer_real(coulomb_upper, shift_next(plane, 1))
        total = total + outer_real(coulomb_lower, shift_prev(plane, 1))
        screened.append(total)
    screened_hat = jnp.fft.fft(screened[0] + 1j * screened[1], axis=0)
    convolved = jnp.fft.ifft(lesser_hat * screened_hat, axis=0)
    sigma_real = -jnp.imag(convolved) * scaling
    sigma_imaginary = jnp.real(convolved) * scaling
    retarded_lower = jnp.swapaxes(shift_prev(retarded_upper, 2), 3, 4)
    out_real, out_imaginary = outer_complex(retarded_diag[0], retarded_diag[1], sigma_real, sigma_imaginary)
    next_real, next_imaginary = outer_complex(retarded_upper[0], retarded_upper[1], shift_next(sigma_real, 1), shift_next(sigma_imaginary, 1))
    prev_real, prev_imaginary = outer_complex(retarded_lower[0], retarded_lower[1], shift_prev(sigma_real, 1), shift_prev(sigma_imaginary, 1))
    out_real = out_real + next_real + prev_real
    out_imaginary = out_imaginary + next_imaginary + prev_imaginary
    return jnp.stack([out_real, out_imaginary]).astype(jnp.float32)
```

```python
import functools
import math

import jax
import jax.numpy as jnp
from jax import lax
from jax.experimental import pallas as pl
from jax.experimental.pallas import tpu as pltpu
from jax.sharding import PartitionSpec as P

MESH = pl.DeviceIdType.MESH
F32, BF16 = jnp.float32, jnp.bfloat16

PLANES = (1, 7, 6, 3, 0, 5, 4, 2)
PAIRS = tuple(PLANES.index(z) for z in range(8))

NE = 32
B = 256
ROWS = B // NE
FACTOR = 1.0 / (math.sqrt(NE) * NE)

GREEN, POL, SCR, SIG = 0, 2, 4, 6
POL_NEXT, SCR_PREV, SIG_NEXT, OUT_PREV, BARE, SPREAD = 8, 9, 10, 11, 12, 13
KINDS = 14


def look_up(values, index):
    packed = sum(v << (3 * i) for i, v in enumerate(values))
    return lax.rem(lax.shift_right_logical(jnp.int32(packed), 3 * index), 8)


def rows_of(r):
    return pl.ds(pl.multiple_of(r * ROWS, ROWS), ROWS)


def split(values):
    high = values.astype(BF16)
    return high, (values - high.astype(F32)).astype(BF16)


def dot3(left, right):
    dot = functools.partial(jnp.dot, preferred_element_type=F32)
    return dot(left[0], right[0]) + dot(left[0], right[1]) + dot(left[1], right[0])


def times_root(real, imaginary, j, half, sign):
    if j == 0:
        return real, imaginary
    if 2 * j == half:
        return (-imaginary, real) if sign > 0 else (imaginary, -real)
    c = math.cos(math.pi * j / half)
    s = sign * math.sin(math.pi * j / half)
    return real * c - imaginary * s, imaginary * c + real * s


def forward(real, imaginary):
    real, imaginary = list(real), list(imaginary)
    half = NE // 2
    while half:
        for first in range(0, NE, 2 * half):
            for j in range(half):
                p, q = first + j, first + j + half
                dr, di = real[p] - real[q], imaginary[p] - imaginary[q]
                real[p], imaginary[p] = real[p] + real[q], imaginary[p] + imaginary[q]
                real[q], imaginary[q] = times_root(dr, di, j, half, -1)
        half //= 2
    return real, imaginary


def inverse(real, imaginary):
    real, imaginary = list(real), list(imaginary)
    half = 1
    while half < NE:
        for first in range(0, NE, 2 * half):
            for j in range(half):
                p, q = first + j, first + j + half
                br, bi = times_root(real[q], imaginary[q], j, half, 1)
                real[q], imaginary[q] = real[p] - br, imaginary[p] - bi
                real[p], imaginary[p] = real[p] + br, imaginary[p] + bi
        half *= 2
    return real, imaginary


def kernel(
    green, retarded_diag, retarded_upper, coulomb_diag, coulomb_upper, out,
    lg, ps, pp, wb, wr, ss, sb, c_send, c_prev, o_send, o_prev, vraw, rraw, ob,
    vh, vl, rh, rl, sh, sl, snd, rcv, loc,
):
    e, d = lax.axis_index("energy"), lax.axis_index("cell")
    zh, x, y = e // 16, (e // 4) % 4, e % 4
    core = d % 2
    z = zh * 4 + d // 2
    r = (x * 4 + y) * 2 + core
    k = look_up(PAIRS, z)
    target = look_up(PLANES, d)

    def at_plane(plane, slot):
        return ((plane // 4) * 16 + slot // 2, (plane % 4) * 2 + slot % 2)

    def slot_at(j):
        return (((x + j // 8) % 4) * 4 + (y + (j // 2) % 4) % 4) * 2 + (core + j % 2) % 2

    def energy_at(j):
        return ((zh + j % 2) % 2) * 16 + ((x + j // 8) % 4) * 4 + (y + (j // 2) % 4) % 4

    def remote(src, dst, kind, device):
        return pltpu.make_async_remote_copy(
            src, dst, snd.at[kind], rcv.at[kind], device_id=device, device_id_type=MESH
        )

    def wait_for(ref, sem):
        pltpu.make_async_copy(ref, ref, sem).wait()

    upper_plane = at_plane(look_up(PLANES, (k + 1) % 8), r)
    lower_plane = at_plane(look_up(PLANES, (k + 7) % 8), r)

    barrier = pltpu.get_barrier_semaphore()

    def greet(device):
        pl.semaphore_signal(barrier, inc=1, device_id=device, device_id_type=MESH)

    @pl.loop(0, NE)
    def _(j):
        greet(at_plane(target, slot_at(j)))
        greet((energy_at(j), k))

    @pl.loop(1, NE)
    def _(j):
        greet(at_plane(z, slot_at(j)))

    pl.when(k < 7)(lambda: greet(upper_plane))
    pl.when(k > 0)(lambda: greet(lower_plane))
    pl.when(d < 7)(lambda: greet((e, d + 1)))
    pl.when(d > 0)(lambda: greet((e, d - 1)))
    expected = 3 * NE - 1 + sum(jnp.where(t, 1, 0) for t in (k < 7, k > 0, d < 7, d > 0))
    pl.semaphore_wait(barrier, expected)

    bare = (x * 4 + y) * 2 + zh
    bare_device = at_plane(target, bare)
    remote(coulomb_diag.at[:, rows_of(bare), :], vraw.at[pl.ds(0, 2), rows_of(bare), :], BARE, bare_device).start()
    remote(coulomb_upper.at[:, rows_of(bare), :], vraw.at[pl.ds(2, 2), rows_of(bare), :], BARE, bare_device).start()

    for c in range(2):

        @pl.loop(0, NE)
        def _(j):
            slot = slot_at(j)
            remote(
                green.at[:, 0, c, rows_of(slot), :], lg.at[c, e], GREEN + c, at_plane(target, slot)
            ).start()

    load_diag = pltpu.make_async_copy(retarded_diag.at[:, 0], rraw.at[0], loc.at[0])
    load_upper = pltpu.make_async_copy(retarded_upper.at[:, 0], rraw.at[1], loc.at[1])
    load_diag.start()
    load_upper.start()

    wait_for(vraw.at[:, pl.ds(0, ROWS), :], rcv.at[BARE])

    @pl.loop(1, NE)
    def _(j):
        remote(
            vraw.at[:, rows_of(r), :], vraw.at[:, rows_of(r), :], SPREAD, at_plane(z, slot_at(j))
        ).start()

    load_diag.wait()
    load_upper.wait()

    @pl.loop(0, 8)
    def _(i):
        kind, plane, c = i // 4, (i // 2) % 2, i % 2
        block = rraw[kind, plane, c]
        at = kind * 4 + c * 2
        rh[at, plane], rl[at, plane] = split(block)
        rh[at + 1, plane], rl[at + 1, plane] = split(block.T)

    wait_for(vraw.at[:, pl.ds(0, B - ROWS), :], rcv.at[SPREAD])

    @pl.loop(0, 2)
    def _(c):
        block = vraw[c]
        vh[c], vl[c] = split((block + block.T) * 0.5)
        block = vraw[2 + c]
        vh[2 + 2 * c], vl[2 + 2 * c] = split(block)
        vh[3 + 2 * c], vl[3 + 2 * c] = split(block.T)

    @pl.loop(0, 2)
    def _(c):
        wait_for(lg.at[c], rcv.at[GREEN + c])

        @pl.loop(0, 2)
        def _(t):
            lanes = pl.ds(pl.multiple_of(t * 128, 128), 128)

            def load(plane):
                return [lg[c, n, plane, :, lanes] for n in range(NE)]

            l_re, l_im = forward(load(0), load(1))
            for n in range(NE):
                lg[c, n, 0, :, lanes] = l_re[n]
                lg[c, n, 1, :, lanes] = l_im[n]
            g_re, g_im = forward(load(2), load(3))
            l_re, l_im = load(0), load(1)
            re = [l_re[n] * g_re[n] + l_im[n] * g_im[n] for n in range(NE)]
            im = [l_im[n] * g_re[n] - l_re[n] * g_im[n] for n in range(NE)]
            re, im = inverse(re, im)
            for n in range(NE):
                ps[c, n, 0, :, lanes] = im[n] * -FACTOR
                ps[c, n, 1, :, lanes] = re[n] * FACTOR

        pltpu.make_async_copy(ps.at[c, r], pp.at[c, :, rows_of(r), :], rcv.at[POL + c]).start()

        @pl.loop(1, NE)
        def _(j):
            slot = slot_at(j)
            remote(
                ps.at[c, slot], pp.at[c, :, rows_of(r), :], POL + c, at_plane(z, slot)
            ).start()

    def screen(first, last, source, plane):
        inner = dot3((vh[first], vl[first]), split(pp[source, plane]))
        return dot3(split(inner), (vh[last], vl[last]))

    wait_for(pp.at[0], rcv.at[POL])
    pol_next = remote(pp.at[0], pp.at[2], POL_NEXT, lower_plane)
    pl.when(k > 0)(pol_next.start)

    @pl.loop(0, 2)
    def _(q):
        wb[0, q] = screen(0, 0, 0, q)
        wb[1, q] = screen(3, 2, 0, q)

    wait_for(pp.at[1], rcv.at[POL + 1])

    @pl.loop(0, 2)
    def _(q):
        c_send[q] = screen(5, 4, 1, q)

    scr_prev = remote(c_send, c_prev, SCR_PREV, upper_plane)
    pl.when(k < 7)(scr_prev.start)

    @pl.loop(0, 2)
    def _(q):
        wb[1, q] += screen(1, 1, 1, q)
        wb[0, q] += screen(2, 3, 1, q)

    def send_screened(c):
        pltpu.make_async_copy(wb.at[c, :, rows_of(r), :], wr.at[c, r], rcv.at[SCR + c]).start()

        @pl.loop(1, NE)
        def _(j):
            slot = slot_at(j)
            remote(
                wb.at[c, :, rows_of(slot), :], wr.at[c, r], SCR + c, at_plane(z, slot)
            ).start()

    @pl.when(k < 7)
    def _():
        wait_for(pp.at[2], rcv.at[POL_NEXT])

        @pl.loop(0, 2)
        def _(q):
            wb[1, q] += screen(4, 5, 2, q)

    send_screened(1)

    @pl.when(k > 0)
    def _():
        wait_for(c_prev, rcv.at[SCR_PREV])
        wb[0] += c_prev[...]

    send_screened(0)

    @pl.loop(0, 2)
    def _(i):
        c = 1 - i
        wait_for(wr.at[c], rcv.at[SCR + c])

        @pl.loop(0, 2)
        def _(t):
            lanes = pl.ds(pl.multiple_of(t * 128, 128), 128)
            w_re, w_im = forward(
                [wr[c, n, 0, :, lanes] for n in range(NE)],
                [wr[c, n, 1, :, lanes] for n in range(NE)],
            )
            l_re = [lg[c, n, 0, :, lanes] for n in range(NE)]
            l_im = [lg[c, n, 1, :, lanes] for n in range(NE)]
            re = [l_re[n] * w_re[n] - l_im[n] * w_im[n] for n in range(NE)]
            im = [l_re[n] * w_im[n] + l_im[n] * w_re[n] for n in range(NE)]
            re, im = inverse(re, im)
            for n in range(NE):
                ss[c, n, 0, :, lanes] = im[n] * -FACTOR
                ss[c, n, 1, :, lanes] = re[n] * FACTOR

        @pl.loop(0, NE)
        def _(j):
            n = energy_at(j)
            remote(ss.at[c, n], sb.at[c, :, rows_of(r), :], SIG + c, (n, k)).start()

    def split_sigma(s):
        @pl.loop(0, 2)
        def _(q):
            sh[q], sl[q] = split(sb[s, q])

    def dress(left, right, half):
        rows = pl.ds(pl.multiple_of(half * 128, 128), 128)
        l_re = (rh[left, 0, rows], rl[left, 0, rows])
        l_im = (rh[left, 1, rows], rl[left, 1, rows])
        s_re, s_im = (sh[0], sl[0]), (sh[1], sl[1])
        t_re = split(dot3(l_re, s_re) - dot3(l_im, s_im))
        t_im = split(dot3(l_re, s_im) + dot3(l_im, s_re))
        b_re = (rh[right, 0], rl[right, 0])
        b_im = (rh[right, 1], rl[right, 1])
        return rows, dot3(t_re, b_re) + dot3(t_im, b_im), dot3(t_im, b_re) - dot3(t_re, b_im)

    wait_for(sb.at[1], rcv.at[SIG + 1])
    split_sigma(1)

    @pl.loop(0, 2)
    def _(half):
        rows, re, im = dress(7, 6, half)
        o_send[0, rows] = re
        o_send[1, rows] = im

    out_prev = remote(o_send, o_prev, OUT_PREV, (e, (d + 1) % 8))
    pl.when(d < 7)(out_prev.start)

    @pl.loop(0, 4)
    def _(i):
        c, half = 1 - i // 2, i % 2
        rows, re, im = dress(2 + 2 * (i // 2), 3 + 2 * (i // 2), half)
        ob[0, c, rows] = re
        ob[1, c, rows] = im

    wait_for(sb.at[0], rcv.at[SIG])
    sig_next = remote(sb.at[0], sb.at[2], SIG_NEXT, (e, (d + 7) % 8))
    pl.when(d > 0)(sig_next.start)
    split_sigma(0)

    @pl.loop(0, 4)
    def _(i):
        c, half = i // 2, i % 2
        rows, re, im = dress(5 * c, 1 + 3 * c, half)
        ob[0, c, rows] += re
        ob[1, c, rows] += im

    @pl.when(d > 0)
    def _():
        wait_for(o_prev, rcv.at[OUT_PREV])
        ob[:, 0] += o_prev[...]

    store_a = pltpu.make_async_copy(ob.at[:, 0], out.at[:, 0, 0], loc.at[0])
    store_a.start()

    @pl.when(d < 7)
    def _():
        wait_for(sb.at[2], rcv.at[SIG_NEXT])
        split_sigma(2)

        @pl.loop(0, 2)
        def _(half):
            rows, re, im = dress(6, 7, half)
            ob[0, 1, rows] += re
            ob[1, 1, rows] += im

    store_b = pltpu.make_async_copy(ob.at[:, 1], out.at[:, 0, 1], loc.at[1])
    store_b.start()

    wait_for(vraw.at[:, pl.ds(0, ROWS), :], snd.at[BARE])
    wait_for(vraw.at[:, pl.ds(0, B - ROWS), :], snd.at[SPREAD])
    for c in range(2):
        wait_for(lg.at[c], snd.at[GREEN + c])
        wait_for(ps.at[c, pl.ds(0, NE - 1)], snd.at[POL + c])
        wait_for(wr.at[c, pl.ds(0, NE - 1)], snd.at[SCR + c])
        wait_for(ss.at[c], snd.at[SIG + c])
    pl.when(k > 0)(pol_next.wait_send)
    pl.when(k < 7)(scr_prev.wait_send)
    pl.when(d > 0)(sig_next.wait_send)
    pl.when(d < 7)(out_prev.wait_send)
    store_a.wait()
    store_b.wait()


def per_device(*arrays):
    block = (2, B, B)
    slices = (2, NE, 2, ROWS, B)
    return pl.pallas_call(
        kernel,
        out_shape=jax.ShapeDtypeStruct((2, 1, 2, B, B), F32),
        in_specs=[pl.BlockSpec(memory_space=pl.ANY)] * 5,
        out_specs=pl.BlockSpec(memory_space=pl.ANY),
        scratch_shapes=[
            pltpu.VMEM((2, NE, 4, ROWS, B), F32),
            pltpu.VMEM(slices, F32),
            pltpu.VMEM((3,) + block, F32),
            pltpu.VMEM((2,) + block, F32),
            pltpu.VMEM(slices, F32),
            pltpu.VMEM(slices, F32),
            pltpu.VMEM((3,) + block, F32),
            pltpu.VMEM(block, F32),
            pltpu.VMEM(block, F32),
            pltpu.VMEM(block, F32),
            pltpu.VMEM(block, F32),
            pltpu.VMEM((4, B, B), F32),
            pltpu.VMEM((2, 2) + block, F32),
            pltpu.VMEM((2,) + block, F32),
            pltpu.VMEM((6, B, B), BF16),
            pltpu.VMEM((6, B, B), BF16),
            pltpu.VMEM((8,) + block, BF16),
            pltpu.VMEM((8,) + block, BF16),
            pltpu.VMEM(block, BF16),
            pltpu.VMEM(block, BF16),
            pltpu.SemaphoreType.DMA((KINDS,)),
            pltpu.SemaphoreType.DMA((KINDS,)),
            pltpu.SemaphoreType.DMA((2,)),
        ],
        compiler_params=pltpu.CompilerParams(
            collective_id=0, has_side_effects=True, vmem_limit_bytes=56 << 20
        ),
        name="self_energy",
    )(*arrays)


def solution(mesh):
    in_specs = (
        P(None, "energy", "cell", None, None),
        P(None, "energy", "cell", None, None),
        P(None, "energy", "cell", None, None),
        P("cell", None, None),
        P("cell", None, None),
    )
    out_specs = P(None, "energy", "cell", None, None)
    return jax.shard_map(
        per_device, mesh=mesh, in_specs=in_specs, out_specs=out_specs, check_vma=False
    )
```

```python
import functools
import math

import jax
import jax.numpy as jnp
from jax import lax
from jax.experimental import pallas as pl
from jax.experimental.pallas import tpu as pltpu
from jax.sharding import PartitionSpec as P

MESH = pl.DeviceIdType.MESH
F32, BF16 = jnp.float32, jnp.bfloat16

PLANES = (2, 7, 6, 4, 3, 1, 0, 5)
PAIRS = tuple(PLANES.index(z) for z in range(8))

NE = 32
B = 256
ROWS = B // NE
FACTOR = 1.0 / (math.sqrt(NE) * NE)

GREEN, POL, SCR, SIG = 0, 2, 4, 6
POL_NEXT, SCR_PREV, SIG_NEXT, OUT_PREV, BARE, SPREAD = 8, 9, 10, 11, 12, 13
KINDS = 14


def look_up(values, index):
    packed = sum(v << (3 * i) for i, v in enumerate(values))
    return lax.rem(lax.shift_right_logical(jnp.int32(packed), 3 * index), 8)


def rows_of(r):
    return pl.ds(pl.multiple_of(r * ROWS, ROWS), ROWS)


def split(values):
    high = values.astype(BF16)
    return high, (values - high.astype(F32)).astype(BF16)


def dot3(left, right):
    dot = functools.partial(jnp.dot, preferred_element_type=F32)
    return dot(left[0], right[0]) + dot(left[0], right[1]) + dot(left[1], right[0])


def times_root(real, imaginary, j, half, sign):
    if j == 0:
        return real, imaginary
    if 2 * j == half:
        return (-imaginary, real) if sign > 0 else (imaginary, -real)
    c = math.cos(math.pi * j / half)
    s = sign * math.sin(math.pi * j / half)
    return real * c - imaginary * s, imaginary * c + real * s


def forward(real, imaginary):
    real, imaginary = list(real), list(imaginary)
    half = NE // 2
    while half:
        for first in range(0, NE, 2 * half):
            for j in range(half):
                p, q = first + j, first + j + half
                dr, di = real[p] - real[q], imaginary[p] - imaginary[q]
                real[p], imaginary[p] = real[p] + real[q], imaginary[p] + imaginary[q]
                real[q], imaginary[q] = times_root(dr, di, j, half, -1)
        half //= 2
    return real, imaginary


def inverse(real, imaginary):
    real, imaginary = list(real), list(imaginary)
    half = 1
    while half < NE:
        for first in range(0, NE, 2 * half):
            for j in range(half):
                p, q = first + j, first + j + half
                br, bi = times_root(real[q], imaginary[q], j, half, 1)
                real[q], imaginary[q] = real[p] - br, imaginary[p] - bi
                real[p], imaginary[p] = real[p] + br, imaginary[p] + bi
        half *= 2
    return real, imaginary


def kernel(
    green, retarded_diag, retarded_upper, coulomb_diag, coulomb_upper, out,
    lg, ps, pp, wb, wr, ss, sb, c_send, c_prev, o_send, o_prev, vraw, rraw, ob,
    vh, vl, rh, rl, sh, sl, snd, rcv, loc,
):
    e, d = lax.axis_index("energy"), lax.axis_index("cell")
    zh, x, y = e // 16, (e // 4) % 4, e % 4
    core = d % 2
    z = zh * 4 + d // 2
    r = (x * 4 + y) * 2 + core
    k = look_up(PAIRS, z)
    target = look_up(PLANES, d)

    def cell_at(step):
        return lax.rem(jnp.where(k < 4, 1, 0) + step, 2)

    def own_cell_at(step):
        return lax.rem(jnp.where(d < 4, 1, 0) + step, 2)

    def at_plane(plane, slot):
        return ((plane // 4) * 16 + slot // 2, (plane % 4) * 2 + slot % 2)

    def slot_at(j):
        return (((x + j // 2) % 4) * 4 + (y + j // 2 + j // 8) % 4) * 2 + (core + j) % 2

    def energy_at(j):
        return ((zh + j) % 2) * 16 + ((x + j // 2) % 4) * 4 + (y + j // 2 + j // 8) % 4

    def remote(src, dst, kind, device):
        return pltpu.make_async_remote_copy(
            src, dst, snd.at[kind], rcv.at[kind], device_id=device, device_id_type=MESH
        )

    def wait_for(ref, sem):
        pltpu.make_async_copy(ref, ref, sem).wait()

    upper_plane = at_plane(look_up(PLANES, (k + 1) % 8), r)
    lower_plane = at_plane(look_up(PLANES, (k + 7) % 8), r)

    barrier = pltpu.get_barrier_semaphore()

    def greet(device):
        pl.semaphore_signal(barrier, inc=1, device_id=device, device_id_type=MESH)

    @pl.loop(0, NE)
    def _(j):
        greet(at_plane(target, slot_at(j)))
        greet((energy_at(j), k))

    @pl.loop(1, NE)
    def _(j):
        greet(at_plane(z, slot_at(j)))

    pl.when(k < 7)(lambda: greet(upper_plane))
    pl.when(k > 0)(lambda: greet(lower_plane))
    pl.when(d < 7)(lambda: greet((e, d + 1)))
    pl.when(d > 0)(lambda: greet((e, d - 1)))
    expected = 3 * NE - 1 + sum(jnp.where(t, 1, 0) for t in (k < 7, k > 0, d < 7, d > 0))
    pl.semaphore_wait(barrier, expected)

    bare = (x * 4 + y) * 2 + zh
    bare_device = at_plane(target, bare)
    remote(coulomb_diag.at[:, rows_of(bare), :], vraw.at[pl.ds(0, 2), rows_of(bare), :], BARE, bare_device).start()
    remote(coulomb_upper.at[:, rows_of(bare), :], vraw.at[pl.ds(2, 2), rows_of(bare), :], BARE, bare_device).start()

    for step in range(2):
        c = own_cell_at(step)

        @pl.loop(0, NE)
        def _(j):
            slot = slot_at(j)
            remote(
                green.at[:, 0, c, rows_of(slot), :], lg.at[c, e], GREEN + step, at_plane(target, slot)
            ).start()

    load_diag = pltpu.make_async_copy(retarded_diag.at[:, 0], rraw.at[0], loc.at[0])
    load_upper = pltpu.make_async_copy(retarded_upper.at[:, 0], rraw.at[1], loc.at[1])
    load_diag.start()
    load_upper.start()

    wait_for(vraw.at[:, pl.ds(0, ROWS), :], rcv.at[BARE])

    @pl.loop(1, NE)
    def _(j):
        remote(
            vraw.at[:, rows_of(r), :], vraw.at[:, rows_of(r), :], SPREAD, at_plane(z, slot_at(j))
        ).start()

    load_diag.wait()
    load_upper.wait()

    @pl.loop(0, 8)
    def _(i):
        kind, plane, c = i // 4, (i // 2) % 2, i % 2
        block = rraw[kind, plane, c]
        at = kind * 4 + c * 2
        rh[at, plane], rl[at, plane] = split(block)
        rh[at + 1, plane], rl[at + 1, plane] = split(block.T)

    wb[...] = jnp.zeros_like(wb)
    ob[...] = jnp.zeros_like(ob)

    def polarize(step):
        c = cell_at(step)
        wait_for(lg.at[c], rcv.at[GREEN + step])

        @pl.loop(0, 2)
        def _(t):
            lanes = pl.ds(pl.multiple_of(t * 128, 128), 128)

            def load(plane):
                return [lg[c, n, plane, :, lanes] for n in range(NE)]

            l_re, l_im = forward(load(0), load(1))
            for n in range(NE):
                lg[c, n, 0, :, lanes] = l_re[n]
                lg[c, n, 1, :, lanes] = l_im[n]
            g_re, g_im = forward(load(2), load(3))
            l_re, l_im = load(0), load(1)
            re = [l_re[n] * g_re[n] + l_im[n] * g_im[n] for n in range(NE)]
            im = [l_im[n] * g_re[n] - l_re[n] * g_im[n] for n in range(NE)]
            re, im = inverse(re, im)
            for n in range(NE):
                ps[c, n, 0, :, lanes] = im[n] * -FACTOR
                ps[c, n, 1, :, lanes] = re[n] * FACTOR

            pltpu.make_async_copy(
                ps.at[c, r, :, :, lanes], pp.at[c, :, rows_of(r), lanes], rcv.at[POL + step]
            ).start()

            @pl.loop(1, NE)
            def _(j):
                slot = slot_at(j)
                remote(
                    ps.at[c, slot, :, :, lanes],
                    pp.at[c, :, rows_of(r), lanes],
                    POL + step,
                    at_plane(z, slot),
                ).start()

    def bare_blocks():
        wait_for(vraw.at[:, pl.ds(0, B - ROWS), :], rcv.at[SPREAD])

        @pl.loop(0, 2)
        def _(c):
            block = vraw[c]
            vh[c], vl[c] = split((block + block.T) * 0.5)
            block = vraw[2 + c]
            vh[2 + 2 * c], vl[2 + 2 * c] = split(block)
            vh[3 + 2 * c], vl[3 + 2 * c] = split(block.T)

    def screen(first, last, source, plane):
        inner = dot3((vh[first], vl[first]), split(pp[source, plane]))
        return dot3(split(inner), (vh[last], vl[last]))

    pol_next = remote(pp.at[0], pp.at[2], POL_NEXT, lower_plane)
    scr_prev = remote(c_send, c_prev, SCR_PREV, upper_plane)

    def spread_polarization(step):
        c = cell_at(step)
        wait_for(pp.at[c], rcv.at[POL + step])
        pl.when((c == 0) & (k > 0))(pol_next.start)

        @pl.when((c == 1) & (k < 7))
        def _():
            @pl.loop(0, 2)
            def _(q):
                c_send[q] = screen(5, 4, 1, q)
                remote(c_send.at[q], c_prev.at[q], SCR_PREV, upper_plane).start()

        @pl.loop(0, 2)
        def _(q):
            wb[c, q] += screen(c, c, c, q)
            wb[1 - c, q] += screen(3 - c, 2 + c, c, q)

    @pl.loop(0, 2)
    def _(step):
        polarize(step)
        pl.when(step == 0)(bare_blocks)
        spread_polarization(step)

    @pl.loop(0, 2)
    def _(step):
        c = cell_at(step + 1)

        @pl.when((c == 1) & (k < 7))
        def _():
            wait_for(pp.at[2], rcv.at[POL_NEXT])

            @pl.loop(0, 2)
            def _(q):
                wb[1, q] += screen(4, 5, 2, q)

        @pl.when((c == 0) & (k > 0))
        def _():
            wait_for(c_prev, rcv.at[SCR_PREV])
            wb[0] += c_prev[...]

        pltpu.make_async_copy(wb.at[c, :, rows_of(r), :], wr.at[c, r], rcv.at[SCR + step]).start()

        @pl.loop(1, NE)
        def _(j):
            slot = slot_at(j)
            remote(
                wb.at[c, :, rows_of(slot), :], wr.at[c, r], SCR + step, at_plane(z, slot)
            ).start()

    @pl.loop(0, 2)
    def _(step):
        c = cell_at(step + 1)
        wait_for(wr.at[c], rcv.at[SCR + step])

        @pl.loop(0, 2)
        def _(t):
            lanes = pl.ds(pl.multiple_of(t * 128, 128), 128)
            w_re, w_im = forward(
                [wr[c, n, 0, :, lanes] for n in range(NE)],
                [wr[c, n, 1, :, lanes] for n in range(NE)],
            )
            l_re = [lg[c, n, 0, :, lanes] for n in range(NE)]
            l_im = [lg[c, n, 1, :, lanes] for n in range(NE)]
            re = [l_re[n] * w_re[n] - l_im[n] * w_im[n] for n in range(NE)]
            im = [l_re[n] * w_im[n] + l_im[n] * w_re[n] for n in range(NE)]
            re, im = inverse(re, im)
            for n in range(NE):
                ss[c, n, 0, :, lanes] = im[n] * -FACTOR
                ss[c, n, 1, :, lanes] = re[n] * FACTOR

        @pl.loop(0, NE)
        def _(j):
            n = energy_at(j)
            remote(ss.at[c, n], sb.at[c, :, rows_of(r), :], SIG + step, (n, k)).start()

    def split_sigma(s):
        @pl.loop(0, 2)
        def _(q):
            sh[q], sl[q] = split(sb[s, q])

    def dress(left, right, half):
        rows = pl.ds(pl.multiple_of(half * 128, 128), 128)
        l_re = (rh[left, 0, rows], rl[left, 0, rows])
        l_im = (rh[left, 1, rows], rl[left, 1, rows])
        s_re, s_im = (sh[0], sl[0]), (sh[1], sl[1])
        t_re = split(dot3(l_re, s_re) - dot3(l_im, s_im))
        t_im = split(dot3(l_re, s_im) + dot3(l_im, s_re))
        b_re = (rh[right, 0], rl[right, 0])
        b_im = (rh[right, 1], rl[right, 1])
        return rows, dot3(t_re, b_re) + dot3(t_im, b_im), dot3(t_im, b_re) - dot3(t_re, b_im)

    sig_next = remote(sb.at[0], sb.at[2], SIG_NEXT, (e, (d + 7) % 8))
    out_prev = remote(o_send, o_prev, OUT_PREV, (e, (d + 1) % 8))

    @pl.loop(0, 2)
    def _(step):
        c = own_cell_at(step + 1)
        wait_for(sb.at[c], rcv.at[SIG + step])
        pl.when((c == 0) & (d > 0))(sig_next.start)
        split_sigma(c)

        @pl.when((c == 1) & (d < 7))
        def _():
            @pl.loop(0, 2)
            def _(half):
                rows, re, im = dress(7, 6, half)
                o_send[0, rows] = re
                o_send[1, rows] = im
                remote(o_send.at[:, rows], o_prev.at[:, rows], OUT_PREV, (e, (d + 1) % 8)).start()

        @pl.loop(0, 4)
        def _(i):
            to, half = (c + i // 2) % 2, i % 2
            other = i // 2
            rows, re, im = dress(2 * c + other * (5 - 3 * c), 2 * c + 1 + other * (3 - c), half)
            ob[0, to, rows] += re
            ob[1, to, rows] += im

    @pl.loop(0, 2)
    def _(step):
        c = own_cell_at(step)

        @pl.when((c == 0) & (d > 0))
        def _():
            wait_for(o_prev, rcv.at[OUT_PREV])
            ob[:, 0] += o_prev[...]

        @pl.when((c == 1) & (d < 7))
        def _():
            wait_for(sb.at[2], rcv.at[SIG_NEXT])
            split_sigma(2)

            @pl.loop(0, 2)
            def _(half):
                rows, re, im = dress(6, 7, half)
                ob[0, 1, rows] += re
                ob[1, 1, rows] += im

        pltpu.make_async_copy(ob.at[:, c], out.at[:, 0, c], loc.at[step]).start()

    wait_for(vraw.at[:, pl.ds(0, ROWS), :], snd.at[BARE])
    wait_for(vraw.at[:, pl.ds(0, B - ROWS), :], snd.at[SPREAD])
    for c in range(2):
        wait_for(lg.at[c], snd.at[GREEN + c])
        wait_for(ps.at[c, pl.ds(0, NE - 1)], snd.at[POL + c])
        wait_for(wr.at[c, pl.ds(0, NE - 1)], snd.at[SCR + c])
        wait_for(ss.at[c], snd.at[SIG + c])
    pl.when(k > 0)(pol_next.wait_send)
    pl.when(k < 7)(scr_prev.wait_send)
    pl.when(d > 0)(sig_next.wait_send)
    pl.when(d < 7)(out_prev.wait_send)
    for step in range(2):
        wait_for(ob.at[:, step], loc.at[step])


def per_device(*arrays):
    block = (2, B, B)
    slices = (2, NE, 2, ROWS, B)
    return pl.pallas_call(
        kernel,
        out_shape=jax.ShapeDtypeStruct((2, 1, 2, B, B), F32),
        in_specs=[pl.BlockSpec(memory_space=pl.ANY)] * 5,
        out_specs=pl.BlockSpec(memory_space=pl.ANY),
        scratch_shapes=[
            pltpu.VMEM((2, NE, 4, ROWS, B), F32),
            pltpu.VMEM(slices, F32),
            pltpu.VMEM((3,) + block, F32),
            pltpu.VMEM((2,) + block, F32),
            pltpu.VMEM(slices, F32),
            pltpu.VMEM(slices, F32),
            pltpu.VMEM((3,) + block, F32),
            pltpu.VMEM(block, F32),
            pltpu.VMEM(block, F32),
            pltpu.VMEM(block, F32),
            pltpu.VMEM(block, F32),
            pltpu.VMEM((4, B, B), F32),
            pltpu.VMEM((2, 2) + block, F32),
            pltpu.VMEM((2,) + block, F32),
            pltpu.VMEM((6, B, B), BF16),
            pltpu.VMEM((6, B, B), BF16),
            pltpu.VMEM((8,) + block, BF16),
            pltpu.VMEM((8,) + block, BF16),
            pltpu.VMEM(block, BF16),
            pltpu.VMEM(block, BF16),
            pltpu.SemaphoreType.DMA((KINDS,)),
            pltpu.SemaphoreType.DMA((KINDS,)),
            pltpu.SemaphoreType.DMA((2,)),
        ],
        compiler_params=pltpu.CompilerParams(
            collective_id=0, has_side_effects=True, vmem_limit_bytes=56 << 20
        ),
        name="self_energy",
    )(*arrays)


def solution(mesh):
    in_specs = (
        P(None, "energy", "cell", None, None),
        P(None, "energy", "cell", None, None),
        P(None, "energy", "cell", None, None),
        P("cell", None, None),
        P("cell", None, None),
    )
    out_specs = P(None, "energy", "cell", None, None)
    return jax.shard_map(
        per_device, mesh=mesh, in_specs=in_specs, out_specs=out_specs, check_vma=False
    )
```

```python
import functools
import math

import jax
import jax.numpy as jnp
from jax import lax
from jax.experimental import pallas as pl
from jax.experimental.pallas import tpu as pltpu
from jax.sharding import PartitionSpec as P

MESH = pl.DeviceIdType.MESH
F32, BF16 = jnp.float32, jnp.bfloat16

PLANES = (2, 7, 6, 4, 3, 1, 0, 5)
PAIRS = tuple(PLANES.index(z) for z in range(8))

NE = 32
B = 256
ROWS = B // NE
FACTOR = 1.0 / (math.sqrt(NE) * NE)

GREEN, POL, SCR, SIG = 0, 2, 4, 6
POL_NEXT, SCR_PREV, SIG_NEXT, OUT_PREV, BARE, SPREAD = 8, 9, 10, 11, 12, 13
KINDS = 14


def look_up(values, index):
    packed = sum(v << (3 * i) for i, v in enumerate(values))
    return lax.rem(lax.shift_right_logical(jnp.int32(packed), 3 * index), 8)


def rows_of(r):
    return pl.ds(pl.multiple_of(r * ROWS, ROWS), ROWS)


def split(values):
    high = values.astype(BF16)
    return high, (values - high.astype(F32)).astype(BF16)


def dot3(left, right):
    dot = functools.partial(jnp.dot, preferred_element_type=F32)
    return dot(left[0], right[0]) + dot(left[0], right[1]) + dot(left[1], right[0])


def times_root(real, imaginary, j, half, sign):
    if j == 0:
        return real, imaginary
    if 2 * j == half:
        return (-imaginary, real) if sign > 0 else (imaginary, -real)
    c = math.cos(math.pi * j / half)
    s = sign * math.sin(math.pi * j / half)
    return real * c - imaginary * s, imaginary * c + real * s


def forward(real, imaginary):
    real, imaginary = list(real), list(imaginary)
    half = NE // 2
    while half:
        for first in range(0, NE, 2 * half):
            for j in range(half):
                p, q = first + j, first + j + half
                dr, di = real[p] - real[q], imaginary[p] - imaginary[q]
                real[p], imaginary[p] = real[p] + real[q], imaginary[p] + imaginary[q]
                real[q], imaginary[q] = times_root(dr, di, j, half, -1)
        half //= 2
    return real, imaginary


def inverse(real, imaginary):
    real, imaginary = list(real), list(imaginary)
    half = 1
    while half < NE:
        for first in range(0, NE, 2 * half):
            for j in range(half):
                p, q = first + j, first + j + half
                br, bi = times_root(real[q], imaginary[q], j, half, 1)
                real[q], imaginary[q] = real[p] - br, imaginary[p] - bi
                real[p], imaginary[p] = real[p] + br, imaginary[p] + bi
        half *= 2
    return real, imaginary


def kernel(
    green, retarded_diag, retarded_upper, coulomb_diag, coulomb_upper, out,
    lg, ps, pp, wb, wr, ss, sb, c_send, c_prev, o_send, o_prev, vraw, rraw, ob,
    vh, vl, rh, rl, sh, sl, snd, rcv, loc,
):
    e, d = lax.axis_index("energy"), lax.axis_index("cell")
    zh, x, y = e // 16, (e // 4) % 4, e % 4
    core = d % 2
    z = zh * 4 + d // 2
    r = (x * 4 + y) * 2 + core
    k = look_up(PAIRS, z)
    target = look_up(PLANES, d)

    def cell_at(step):
        return lax.rem(jnp.where(k < 4, 1, 0) + step, 2)

    def own_cell_at(step):
        return lax.rem(jnp.where(d < 4, 1, 0) + step, 2)

    def at_plane(plane, slot):
        return ((plane // 4) * 16 + slot // 2, (plane % 4) * 2 + slot % 2)

    turn = 16 * core + 8 * (z % 2)

    def slot_at(j):
        j = j % NE
        return (((x + j // 2) % 4) * 4 + (y + j // 2 + j // 8) % 4) * 2 + (core + j) % 2

    def energy_at(j):
        j = j % NE
        return ((zh + j) % 2) * 16 + ((x + j // 2) % 4) * 4 + (y + j // 2 + j // 8) % 4

    def remote(src, dst, kind, device):
        return pltpu.make_async_remote_copy(
            src, dst, snd.at[kind], rcv.at[kind], device_id=device, device_id_type=MESH
        )

    def wait_for(ref, sem):
        pltpu.make_async_copy(ref, ref, sem).wait()

    upper_plane = at_plane(look_up(PLANES, (k + 1) % 8), r)
    lower_plane = at_plane(look_up(PLANES, (k + 7) % 8), r)

    barrier = pltpu.get_barrier_semaphore()

    def greet(device):
        pl.semaphore_signal(barrier, inc=1, device_id=device, device_id_type=MESH)

    @pl.loop(0, NE)
    def _(j):
        greet(at_plane(target, slot_at(j)))
        greet((energy_at(j), k))

    @pl.loop(1, NE)
    def _(j):
        greet(at_plane(z, slot_at(j)))

    pl.when(k < 7)(lambda: greet(upper_plane))
    pl.when(k > 0)(lambda: greet(lower_plane))
    pl.when(d < 7)(lambda: greet((e, d + 1)))
    pl.when(d > 0)(lambda: greet((e, d - 1)))
    expected = 3 * NE - 1 + sum(jnp.where(t, 1, 0) for t in (k < 7, k > 0, d < 7, d > 0))
    pl.semaphore_wait(barrier, expected)

    bare = (x * 4 + y) * 2 + zh
    bare_device = at_plane(target, bare)
    remote(coulomb_diag.at[:, rows_of(bare), :], vraw.at[pl.ds(0, 2), rows_of(bare), :], BARE, bare_device).start()
    remote(coulomb_upper.at[:, rows_of(bare), :], vraw.at[pl.ds(2, 2), rows_of(bare), :], BARE, bare_device).start()

    for step in range(2):
        c = own_cell_at(step)

        @pl.loop(0, NE)
        def _(j):
            slot = slot_at(j + turn)
            remote(
                green.at[:, 0, c, rows_of(slot), :], lg.at[c, e], GREEN + step, at_plane(target, slot)
            ).start()

    load_diag = pltpu.make_async_copy(retarded_diag.at[:, 0], rraw.at[0], loc.at[0])
    load_upper = pltpu.make_async_copy(retarded_upper.at[:, 0], rraw.at[1], loc.at[1])
    load_diag.start()
    load_upper.start()

    wait_for(vraw.at[:, pl.ds(0, ROWS), :], rcv.at[BARE])

    @pl.loop(1, NE)
    def _(j):
        remote(
            vraw.at[:, rows_of(r), :], vraw.at[:, rows_of(r), :], SPREAD, at_plane(z, slot_at(1 + (j - 1 + turn) % (NE - 1)))
        ).start()

    load_diag.wait()
    load_upper.wait()

    @pl.loop(0, 8)
    def _(i):
        kind, plane, c = i // 4, (i // 2) % 2, i % 2
        block = rraw[kind, plane, c]
        at = kind * 4 + c * 2
        rh[at, plane], rl[at, plane] = split(block)
        rh[at + 1, plane], rl[at + 1, plane] = split(block.T)

    wb[...] = jnp.zeros_like(wb)
    ob[...] = jnp.zeros_like(ob)

    def polarize(step):
        c = cell_at(step)
        wait_for(lg.at[c], rcv.at[GREEN + step])

        @pl.loop(0, 2)
        def _(t):
            lanes = pl.ds(pl.multiple_of(t * 128, 128), 128)

            def load(plane):
                return [lg[c, n, plane, :, lanes] for n in range(NE)]

            l_re, l_im = forward(load(0), load(1))
            for n in range(NE):
                lg[c, n, 0, :, lanes] = l_re[n]
                lg[c, n, 1, :, lanes] = l_im[n]
            g_re, g_im = forward(load(2), load(3))
            l_re, l_im = load(0), load(1)
            re = [l_re[n] * g_re[n] + l_im[n] * g_im[n] for n in range(NE)]
            im = [l_im[n] * g_re[n] - l_re[n] * g_im[n] for n in range(NE)]
            re, im = inverse(re, im)
            for n in range(NE):
                ps[c, n, 0, :, lanes] = im[n] * -FACTOR
                ps[c, n, 1, :, lanes] = re[n] * FACTOR

            pltpu.make_async_copy(
                ps.at[c, r, :, :, lanes], pp.at[c, :, rows_of(r), lanes], rcv.at[POL + step]
            ).start()

            @pl.loop(1, NE)
            def _(j):
                slot = slot_at(1 + (j - 1 + turn) % (NE - 1))
                remote(
                    ps.at[c, slot, :, :, lanes],
                    pp.at[c, :, rows_of(r), lanes],
                    POL + step,
                    at_plane(z, slot),
                ).start()

    def bare_blocks():
        wait_for(vraw.at[:, pl.ds(0, B - ROWS), :], rcv.at[SPREAD])

        @pl.loop(0, 2)
        def _(c):
            block = vraw[c]
            vh[c], vl[c] = split((block + block.T) * 0.5)
            block = vraw[2 + c]
            vh[2 + 2 * c], vl[2 + 2 * c] = split(block)
            vh[3 + 2 * c], vl[3 + 2 * c] = split(block.T)

    def screen(first, last, source, plane):
        inner = dot3((vh[first], vl[first]), split(pp[source, plane]))
        return dot3(split(inner), (vh[last], vl[last]))

    pol_next = remote(pp.at[0], pp.at[2], POL_NEXT, lower_plane)
    scr_prev = remote(c_send, c_prev, SCR_PREV, upper_plane)

    def spread_polarization(step):
        c = cell_at(step)
        wait_for(pp.at[c], rcv.at[POL + step])
        pl.when((c == 0) & (k > 0))(pol_next.start)

        @pl.when((c == 1) & (k < 7))
        def _():
            @pl.loop(0, 2)
            def _(q):
                c_send[q] = screen(5, 4, 1, q)
                remote(c_send.at[q], c_prev.at[q], SCR_PREV, upper_plane).start()

        @pl.loop(0, 2)
        def _(q):
            wb[c, q] += screen(c, c, c, q)
            wb[1 - c, q] += screen(3 - c, 2 + c, c, q)

    @pl.loop(0, 2)
    def _(step):
        polarize(step)
        pl.when(step == 0)(bare_blocks)
        spread_polarization(step)

    @pl.loop(0, 2)
    def _(step):
        c = cell_at(step + 1)

        @pl.when((c == 1) & (k < 7))
        def _():
            wait_for(pp.at[2], rcv.at[POL_NEXT])

            @pl.loop(0, 2)
            def _(q):
                wb[1, q] += screen(4, 5, 2, q)

        @pl.when((c == 0) & (k > 0))
        def _():
            wait_for(c_prev, rcv.at[SCR_PREV])
            wb[0] += c_prev[...]

        pltpu.make_async_copy(wb.at[c, :, rows_of(r), :], wr.at[c, r], rcv.at[SCR + step]).start()

        @pl.loop(1, NE)
        def _(j):
            slot = slot_at(1 + (j - 1 + turn) % (NE - 1))
            remote(
                wb.at[c, :, rows_of(slot), :], wr.at[c, r], SCR + step, at_plane(z, slot)
            ).start()

    @pl.loop(0, 2)
    def _(step):
        c = cell_at(step + 1)
        wait_for(wr.at[c], rcv.at[SCR + step])

        @pl.loop(0, 2)
        def _(t):
            lanes = pl.ds(pl.multiple_of(t * 128, 128), 128)
            w_re, w_im = forward(
                [wr[c, n, 0, :, lanes] for n in range(NE)],
                [wr[c, n, 1, :, lanes] for n in range(NE)],
            )
            l_re = [lg[c, n, 0, :, lanes] for n in range(NE)]
            l_im = [lg[c, n, 1, :, lanes] for n in range(NE)]
            re = [l_re[n] * w_re[n] - l_im[n] * w_im[n] for n in range(NE)]
            im = [l_re[n] * w_im[n] + l_im[n] * w_re[n] for n in range(NE)]
            re, im = inverse(re, im)
            for n in range(NE):
                ss[c, n, 0, :, lanes] = im[n] * -FACTOR
                ss[c, n, 1, :, lanes] = re[n] * FACTOR

        @pl.loop(0, NE)
        def _(j):
            n = energy_at(j + turn)
            remote(ss.at[c, n], sb.at[c, :, rows_of(r), :], SIG + step, (n, k)).start()

    def split_sigma(s):
        @pl.loop(0, 2)
        def _(q):
            sh[q], sl[q] = split(sb[s, q])

    def dress(left, right, half):
        rows = pl.ds(pl.multiple_of(half * 128, 128), 128)
        l_re = (rh[left, 0, rows], rl[left, 0, rows])
        l_im = (rh[left, 1, rows], rl[left, 1, rows])
        s_re, s_im = (sh[0], sl[0]), (sh[1], sl[1])
        t_re = split(dot3(l_re, s_re) - dot3(l_im, s_im))
        t_im = split(dot3(l_re, s_im) + dot3(l_im, s_re))
        b_re = (rh[right, 0], rl[right, 0])
        b_im = (rh[right, 1], rl[right, 1])
        return rows, dot3(t_re, b_re) + dot3(t_im, b_im), dot3(t_im, b_re) - dot3(t_re, b_im)

    sig_next = remote(sb.at[0], sb.at[2], SIG_NEXT, (e, (d + 7) % 8))
    out_prev = remote(o_send, o_prev, OUT_PREV, (e, (d + 1) % 8))

    @pl.loop(0, 2)
    def _(step):
        c = own_cell_at(step + 1)
        wait_for(sb.at[c], rcv.at[SIG + step])
        pl.when((c == 0) & (d > 0))(sig_next.start)
        split_sigma(c)

        @pl.when((c == 1) & (d < 7))
        def _():
            @pl.loop(0, 2)
            def _(half):
                rows, re, im = dress(7, 6, half)
                o_send[0, rows] = re
                o_send[1, rows] = im
                remote(o_send.at[:, rows], o_prev.at[:, rows], OUT_PREV, (e, (d + 1) % 8)).start()

        @pl.loop(0, 4)
        def _(i):
            to, half = (c + i // 2) % 2, i % 2
            other = i // 2
            rows, re, im = dress(2 * c + other * (5 - 3 * c), 2 * c + 1 + other * (3 - c), half)
            ob[0, to, rows] += re
            ob[1, to, rows] += im

    @pl.loop(0, 2)
    def _(step):
        c = own_cell_at(step)

        @pl.when((c == 0) & (d > 0))
        def _():
            wait_for(o_prev, rcv.at[OUT_PREV])
            ob[:, 0] += o_prev[...]

        @pl.when((c == 1) & (d < 7))
        def _():
            wait_for(sb.at[2], rcv.at[SIG_NEXT])
            split_sigma(2)

            @pl.loop(0, 2)
            def _(half):
                rows, re, im = dress(6, 7, half)
                ob[0, 1, rows] += re
                ob[1, 1, rows] += im

        pltpu.make_async_copy(ob.at[:, c], out.at[:, 0, c], loc.at[step]).start()

    wait_for(vraw.at[:, pl.ds(0, ROWS), :], snd.at[BARE])
    wait_for(vraw.at[:, pl.ds(0, B - ROWS), :], snd.at[SPREAD])
    for c in range(2):
        wait_for(lg.at[c], snd.at[GREEN + c])
        wait_for(ps.at[c, pl.ds(0, NE - 1)], snd.at[POL + c])
        wait_for(wr.at[c, pl.ds(0, NE - 1)], snd.at[SCR + c])
        wait_for(ss.at[c], snd.at[SIG + c])
    pl.when(k > 0)(pol_next.wait_send)
    pl.when(k < 7)(scr_prev.wait_send)
    pl.when(d > 0)(sig_next.wait_send)
    pl.when(d < 7)(out_prev.wait_send)
    for step in range(2):
        wait_for(ob.at[:, step], loc.at[step])


def per_device(*arrays):
    block = (2, B, B)
    slices = (2, NE, 2, ROWS, B)
    return pl.pallas_call(
        kernel,
        out_shape=jax.ShapeDtypeStruct((2, 1, 2, B, B), F32),
        in_specs=[pl.BlockSpec(memory_space=pl.ANY)] * 5,
        out_specs=pl.BlockSpec(memory_space=pl.ANY),
        scratch_shapes=[
            pltpu.VMEM((2, NE, 4, ROWS, B), F32),
            pltpu.VMEM(slices, F32),
            pltpu.VMEM((3,) + block, F32),
            pltpu.VMEM((2,) + block, F32),
            pltpu.VMEM(slices, F32),
            pltpu.VMEM(slices, F32),
            pltpu.VMEM((3,) + block, F32),
            pltpu.VMEM(block, F32),
            pltpu.VMEM(block, F32),
            pltpu.VMEM(block, F32),
            pltpu.VMEM(block, F32),
            pltpu.VMEM((4, B, B), F32),
            pltpu.VMEM((2, 2) + block, F32),
            pltpu.VMEM((2,) + block, F32),
            pltpu.VMEM((6, B, B), BF16),
            pltpu.VMEM((6, B, B), BF16),
            pltpu.VMEM((8,) + block, BF16),
            pltpu.VMEM((8,) + block, BF16),
            pltpu.VMEM(block, BF16),
            pltpu.VMEM(block, BF16),
            pltpu.SemaphoreType.DMA((KINDS,)),
            pltpu.SemaphoreType.DMA((KINDS,)),
            pltpu.SemaphoreType.DMA((2,)),
        ],
        compiler_params=pltpu.CompilerParams(
            collective_id=0, has_side_effects=True, vmem_limit_bytes=56 << 20
        ),
        name="self_energy",
    )(*arrays)


def solution(mesh):
    in_specs = (
        P(None, "energy", "cell", None, None),
        P(None, "energy", "cell", None, None),
        P(None, "energy", "cell", None, None),
        P("cell", None, None),
        P("cell", None, None),
    )
    out_specs = P(None, "energy", "cell", None, None)
    return jax.shard_map(
        per_device, mesh=mesh, in_specs=in_specs, out_specs=out_specs, check_vma=False
    )
```

```python
import functools
import math

import jax
import jax.numpy as jnp
from jax import lax
from jax.experimental import pallas as pl
from jax.experimental.pallas import tpu as pltpu
from jax.sharding import PartitionSpec as P

MESH = pl.DeviceIdType.MESH
F32, BF16 = jnp.float32, jnp.bfloat16

PLANES = (2, 7, 6, 4, 3, 1, 0, 5)
PAIRS = tuple(PLANES.index(z) for z in range(8))

NE = 32
B = 256
ROWS = B // NE
FACTOR = 1.0 / (math.sqrt(NE) * NE)

GREEN, POL, SCR, SIG = 0, 2, 4, 6
POL_NEXT, SCR_PREV, SIG_NEXT, OUT_PREV, BARE, SPREAD = 8, 9, 10, 11, 12, 13
KINDS = 14


def look_up(values, index):
    packed = sum(v << (3 * i) for i, v in enumerate(values))
    return lax.rem(lax.shift_right_logical(jnp.int32(packed), 3 * index), 8)


def rows_of(r):
    return pl.ds(pl.multiple_of(r * ROWS, ROWS), ROWS)


def split(values):
    high = values.astype(BF16)
    return high, (values - high.astype(F32)).astype(BF16)


def dot3(left, right):
    dot = functools.partial(jnp.dot, preferred_element_type=F32)
    return dot(left[0], right[0]) + dot(left[0], right[1]) + dot(left[1], right[0])


def times_root(real, imaginary, j, half, sign):
    if j == 0:
        return real, imaginary
    if 2 * j == half:
        return (-imaginary, real) if sign > 0 else (imaginary, -real)
    c = math.cos(math.pi * j / half)
    s = sign * math.sin(math.pi * j / half)
    return real * c - imaginary * s, imaginary * c + real * s


def forward(real, imaginary):
    real, imaginary = list(real), list(imaginary)
    half = NE // 2
    while half:
        for first in range(0, NE, 2 * half):
            for j in range(half):
                p, q = first + j, first + j + half
                dr, di = real[p] - real[q], imaginary[p] - imaginary[q]
                real[p], imaginary[p] = real[p] + real[q], imaginary[p] + imaginary[q]
                real[q], imaginary[q] = times_root(dr, di, j, half, -1)
        half //= 2
    return real, imaginary


def inverse(real, imaginary):
    real, imaginary = list(real), list(imaginary)
    half = 1
    while half < NE:
        for first in range(0, NE, 2 * half):
            for j in range(half):
                p, q = first + j, first + j + half
                br, bi = times_root(real[q], imaginary[q], j, half, 1)
                real[q], imaginary[q] = real[p] - br, imaginary[p] - bi
                real[p], imaginary[p] = real[p] + br, imaginary[p] + bi
        half *= 2
    return real, imaginary


def kernel(
    green, retarded_diag, retarded_upper, coulomb_diag, coulomb_upper, out,
    lg, ps, pp, wb, wr, ss, sb, c_send, c_prev, o_send, o_prev, vraw, rraw, ob,
    vh, vl, rh, rl, sh, sl, snd, rcv, loc,
):
    e, d = lax.axis_index("energy"), lax.axis_index("cell")
    zh, x, y = e // 16, (e // 4) % 4, e % 4
    core = d % 2
    z = zh * 4 + d // 2
    r = (x * 4 + y) * 2 + core
    k = look_up(PAIRS, z)
    target = look_up(PLANES, d)

    def cell_at(step):
        return lax.rem(jnp.where(k < 4, 1, 0) + step, 2)

    def own_cell_at(step):
        return lax.rem(jnp.where(d < 4, 1, 0) + step, 2)

    def at_plane(plane, slot):
        return ((plane // 4) * 16 + slot // 2, (plane % 4) * 2 + slot % 2)

    turn = 16 * core + 8 * (z % 2)

    def slot_at(j):
        j = j % NE
        return (((x + j // 2) % 4) * 4 + (y + j // 2 + j // 8) % 4) * 2 + (core + j) % 2

    def energy_at(j):
        j = j % NE
        return ((zh + j) % 2) * 16 + ((x + j // 2) % 4) * 4 + (y + j // 2 + j // 8) % 4

    def remote(src, dst, kind, device):
        return pltpu.make_async_remote_copy(
            src, dst, snd.at[kind], rcv.at[kind], device_id=device, device_id_type=MESH
        )

    def wait_for(ref, sem):
        pltpu.make_async_copy(ref, ref, sem).wait()

    upper_plane = at_plane(look_up(PLANES, (k + 1) % 8), r)
    lower_plane = at_plane(look_up(PLANES, (k + 7) % 8), r)

    barrier = pltpu.get_barrier_semaphore()

    def greet(device):
        pl.semaphore_signal(barrier, inc=1, device_id=device, device_id_type=MESH)

    @pl.loop(0, NE)
    def _(j):
        greet(at_plane(target, slot_at(j)))
        greet((energy_at(j), k))

    @pl.loop(1, NE)
    def _(j):
        greet(at_plane(z, slot_at(j)))

    pl.when(k < 7)(lambda: greet(upper_plane))
    pl.when(k > 0)(lambda: greet(lower_plane))
    pl.when(d < 7)(lambda: greet((e, d + 1)))
    pl.when(d > 0)(lambda: greet((e, d - 1)))
    expected = 3 * NE - 1 + sum(jnp.where(t, 1, 0) for t in (k < 7, k > 0, d < 7, d > 0))
    pl.semaphore_wait(barrier, expected)

    bare = (x * 4 + y) * 2 + zh
    bare_device = at_plane(target, bare)
    remote(coulomb_diag.at[:, rows_of(bare), :], vraw.at[pl.ds(0, 2), rows_of(bare), :], BARE, bare_device).start()
    remote(coulomb_upper.at[:, rows_of(bare), :], vraw.at[pl.ds(2, 2), rows_of(bare), :], BARE, bare_device).start()

    for step in range(2):
        c = own_cell_at(step)

        @pl.loop(0, NE)
        def _(j):
            slot = slot_at(j + turn)
            remote(
                green.at[:, 0, c, rows_of(slot), :], lg.at[c, e], GREEN + step, at_plane(target, slot)
            ).start()

    load_diag = pltpu.make_async_copy(retarded_diag.at[:, 0], rraw.at[0], loc.at[0])
    load_upper = pltpu.make_async_copy(retarded_upper.at[:, 0], rraw.at[1], loc.at[1])
    load_diag.start()
    load_upper.start()

    wait_for(vraw.at[:, pl.ds(0, ROWS), :], rcv.at[BARE])

    @pl.loop(1, NE)
    def _(j):
        remote(
            vraw.at[:, rows_of(r), :], vraw.at[:, rows_of(r), :], SPREAD, at_plane(z, slot_at(1 + (j - 1 + turn) % (NE - 1)))
        ).start()

    load_diag.wait()
    load_upper.wait()

    @pl.loop(0, 8)
    def _(i):
        kind, plane, c = i // 4, (i // 2) % 2, i % 2
        block = rraw[kind, plane, c]
        at = kind * 4 + c * 2
        rh[at, plane], rl[at, plane] = split(block)
        rh[at + 1, plane], rl[at + 1, plane] = split(block.T)

    wb[...] = jnp.zeros_like(wb)
    ob[...] = jnp.zeros_like(ob)

    def polarize(step):
        c = cell_at(step)
        wait_for(lg.at[c], rcv.at[GREEN + step])

        @pl.loop(0, 2)
        def _(t):
            lanes = pl.ds(pl.multiple_of(t * 128, 128), 128)

            def load(plane):
                return [lg[c, n, plane, :, lanes] for n in range(NE)]

            l_re, l_im = forward(load(0), load(1))
            for n in range(NE):
                lg[c, n, 0, :, lanes] = l_re[n]
                lg[c, n, 1, :, lanes] = l_im[n]
            g_re, g_im = forward(load(2), load(3))
            l_re, l_im = load(0), load(1)
            re = [l_re[n] * g_re[n] + l_im[n] * g_im[n] for n in range(NE)]
            im = [l_im[n] * g_re[n] - l_re[n] * g_im[n] for n in range(NE)]
            re, im = inverse(re, im)
            for n in range(NE):
                ps[c, n, 0, :, lanes] = im[n] * -FACTOR
                ps[c, n, 1, :, lanes] = re[n] * FACTOR

            pltpu.make_async_copy(
                ps.at[c, r, :, :, lanes], pp.at[c, :, rows_of(r), lanes], rcv.at[POL + step]
            ).start()

            @pl.loop(1, NE)
            def _(j):
                slot = slot_at(1 + (j - 1 + turn) % (NE - 1))
                remote(
                    ps.at[c, slot, :, :, lanes],
                    pp.at[c, :, rows_of(r), lanes],
                    POL + step,
                    at_plane(z, slot),
                ).start()

    def bare_blocks():
        wait_for(vraw.at[:, pl.ds(0, B - ROWS), :], rcv.at[SPREAD])

        @pl.loop(0, 2)
        def _(c):
            block = vraw[c]
            vh[c], vl[c] = split((block + block.T) * 0.5)
            block = vraw[2 + c]
            vh[2 + 2 * c], vl[2 + 2 * c] = split(block)
            vh[3 + 2 * c], vl[3 + 2 * c] = split(block.T)

    def screen(first, last, source, plane):
        inner = dot3((vh[first], vl[first]), split(pp[source, plane]))
        return dot3(split(inner), (vh[last], vl[last]))

    pol_next = remote(pp.at[0], pp.at[2], POL_NEXT, lower_plane)
    scr_prev = remote(c_send, c_prev, SCR_PREV, upper_plane)

    def spread_polarization(step):
        c = cell_at(step)
        wait_for(pp.at[c], rcv.at[POL + step])
        pl.when((c == 0) & (k > 0))(pol_next.start)

        @pl.when((c == 1) & (k < 7))
        def _():
            @pl.loop(0, 2)
            def _(q):
                c_send[q] = screen(5, 4, 1, q)
                remote(c_send.at[q], c_prev.at[q], SCR_PREV, upper_plane).start()

        @pl.loop(0, 2)
        def _(q):
            wb[c, q] += screen(c, c, c, q)
            wb[1 - c, q] += screen(3 - c, 2 + c, c, q)

    @pl.loop(0, 2)
    def _(step):
        polarize(step)
        pl.when(step == 0)(bare_blocks)
        spread_polarization(step)

    @pl.loop(0, 2)
    def _(step):
        c = cell_at(step + 1)

        @pl.when((c == 1) & (k < 7))
        def _():
            wait_for(pp.at[2], rcv.at[POL_NEXT])

            @pl.loop(0, 2)
            def _(q):
                wb[1, q] += screen(4, 5, 2, q)

        @pl.when((c == 0) & (k > 0))
        def _():
            wait_for(c_prev, rcv.at[SCR_PREV])
            wb[0] += c_prev[...]

        pltpu.make_async_copy(wb.at[c, :, rows_of(r), :], wr.at[c, r], rcv.at[SCR + step]).start()

        @pl.loop(1, NE)
        def _(j):
            slot = slot_at(1 + (j - 1 + turn) % (NE - 1))
            remote(
                wb.at[c, :, rows_of(slot), :], wr.at[c, r], SCR + step, at_plane(z, slot)
            ).start()

    @pl.loop(0, 2)
    def _(step):
        c = cell_at(step + 1)
        wait_for(wr.at[c], rcv.at[SCR + step])

        @pl.loop(0, 2)
        def _(t):
            lanes = pl.ds(pl.multiple_of(t * 128, 128), 128)
            w_re, w_im = forward(
                [wr[c, n, 0, :, lanes] for n in range(NE)],
                [wr[c, n, 1, :, lanes] for n in range(NE)],
            )
            l_re = [lg[c, n, 0, :, lanes] for n in range(NE)]
            l_im = [lg[c, n, 1, :, lanes] for n in range(NE)]
            re = [l_re[n] * w_re[n] - l_im[n] * w_im[n] for n in range(NE)]
            im = [l_re[n] * w_im[n] + l_im[n] * w_re[n] for n in range(NE)]
            re, im = inverse(re, im)
            for n in range(NE):
                ss[c, n, 0, :, lanes] = im[n] * -FACTOR
                ss[c, n, 1, :, lanes] = re[n] * FACTOR

            @pl.loop(0, NE)
            def _(j):
                n = energy_at(j + turn)
                remote(
                    ss.at[c, n, :, :, lanes], sb.at[c, :, rows_of(r), lanes], SIG + step, (n, k)
                ).start()

    def split_sigma(s):
        @pl.loop(0, 2)
        def _(q):
            sh[q], sl[q] = split(sb[s, q])

    def dress(left, right, half):
        rows = pl.ds(pl.multiple_of(half * 128, 128), 128)
        l_re = (rh[left, 0, rows], rl[left, 0, rows])
        l_im = (rh[left, 1, rows], rl[left, 1, rows])
        s_re, s_im = (sh[0], sl[0]), (sh[1], sl[1])
        t_re = split(dot3(l_re, s_re) - dot3(l_im, s_im))
        t_im = split(dot3(l_re, s_im) + dot3(l_im, s_re))
        b_re = (rh[right, 0], rl[right, 0])
        b_im = (rh[right, 1], rl[right, 1])
        return rows, dot3(t_re, b_re) + dot3(t_im, b_im), dot3(t_im, b_re) - dot3(t_re, b_im)

    sig_next = remote(sb.at[0], sb.at[2], SIG_NEXT, (e, (d + 7) % 8))
    out_prev = remote(o_send, o_prev, OUT_PREV, (e, (d + 1) % 8))

    @pl.loop(0, 2)
    def _(step):
        c = own_cell_at(step + 1)
        wait_for(sb.at[c], rcv.at[SIG + step])
        pl.when((c == 0) & (d > 0))(sig_next.start)
        split_sigma(c)

        @pl.when((c == 1) & (d < 7))
        def _():
            @pl.loop(0, 2)
            def _(half):
                rows, re, im = dress(7, 6, half)
                o_send[0, rows] = re
                o_send[1, rows] = im
                remote(o_send.at[:, rows], o_prev.at[:, rows], OUT_PREV, (e, (d + 1) % 8)).start()

        @pl.loop(0, 4)
        def _(i):
            to, half = (c + i // 2) % 2, i % 2
            other = i // 2
            rows, re, im = dress(2 * c + other * (5 - 3 * c), 2 * c + 1 + other * (3 - c), half)
            ob[0, to, rows] += re
            ob[1, to, rows] += im

    @pl.loop(0, 2)
    def _(step):
        c = own_cell_at(step)

        @pl.when((c == 0) & (d > 0))
        def _():
            wait_for(o_prev, rcv.at[OUT_PREV])
            ob[:, 0] += o_prev[...]

        @pl.when((c == 1) & (d < 7))
        def _():
            wait_for(sb.at[2], rcv.at[SIG_NEXT])
            split_sigma(2)

            @pl.loop(0, 2)
            def _(half):
                rows, re, im = dress(6, 7, half)
                ob[0, 1, rows] += re
                ob[1, 1, rows] += im

        pltpu.make_async_copy(ob.at[:, c], out.at[:, 0, c], loc.at[step]).start()

    wait_for(vraw.at[:, pl.ds(0, ROWS), :], snd.at[BARE])
    wait_for(vraw.at[:, pl.ds(0, B - ROWS), :], snd.at[SPREAD])
    for c in range(2):
        wait_for(lg.at[c], snd.at[GREEN + c])
        wait_for(ps.at[c, pl.ds(0, NE - 1)], snd.at[POL + c])
        wait_for(wr.at[c, pl.ds(0, NE - 1)], snd.at[SCR + c])
        wait_for(ss.at[c], snd.at[SIG + c])
    pl.when(k > 0)(pol_next.wait_send)
    pl.when(k < 7)(scr_prev.wait_send)
    pl.when(d > 0)(sig_next.wait_send)
    pl.when(d < 7)(out_prev.wait_send)
    for step in range(2):
        wait_for(ob.at[:, step], loc.at[step])


def per_device(*arrays):
    block = (2, B, B)
    slices = (2, NE, 2, ROWS, B)
    return pl.pallas_call(
        kernel,
        out_shape=jax.ShapeDtypeStruct((2, 1, 2, B, B), F32),
        in_specs=[pl.BlockSpec(memory_space=pl.ANY)] * 5,
        out_specs=pl.BlockSpec(memory_space=pl.ANY),
        scratch_shapes=[
            pltpu.VMEM((2, NE, 4, ROWS, B), F32),
            pltpu.VMEM(slices, F32),
            pltpu.VMEM((3,) + block, F32),
            pltpu.VMEM((2,) + block, F32),
            pltpu.VMEM(slices, F32),
            pltpu.VMEM(slices, F32),
            pltpu.VMEM((3,) + block, F32),
            pltpu.VMEM(block, F32),
            pltpu.VMEM(block, F32),
            pltpu.VMEM(block, F32),
            pltpu.VMEM(block, F32),
            pltpu.VMEM((4, B, B), F32),
            pltpu.VMEM((2, 2) + block, F32),
            pltpu.VMEM((2,) + block, F32),
            pltpu.VMEM((6, B, B), BF16),
            pltpu.VMEM((6, B, B), BF16),
            pltpu.VMEM((8,) + block, BF16),
            pltpu.VMEM((8,) + block, BF16),
            pltpu.VMEM(block, BF16),
            pltpu.VMEM(block, BF16),
            pltpu.SemaphoreType.DMA((KINDS,)),
            pltpu.SemaphoreType.DMA((KINDS,)),
            pltpu.SemaphoreType.DMA((2,)),
        ],
        compiler_params=pltpu.CompilerParams(
            collective_id=0, has_side_effects=True, vmem_limit_bytes=56 << 20
        ),
        name="self_energy",
    )(*arrays)


def solution(mesh):
    in_specs = (
        P(None, "energy", "cell", None, None),
        P(None, "energy", "cell", None, None),
        P(None, "energy", "cell", None, None),
        P("cell", None, None),
        P("cell", None, None),
    )
    out_specs = P(None, "energy", "cell", None, None)
    return jax.shard_map(
        per_device, mesh=mesh, in_specs=in_specs, out_specs=out_specs, check_vma=False
    )
```
